512 devices in a mesh: track: 8 (over y, core), pix: 64 (over z, x).
Axes of the slice: x: 4, y: 4, z: 16, core: 2. Of those that a mesh axis runs over, the one named last changes fastest.
Arguments:
- phases: bfloat16 [8, 256, 524288], P('track', 'pix'), may hold values from -15 to 15
- coherent: int32 [8, 256, 4096], P('track', 'pix'), may hold values 0 or 1
- pairs: int32 [8, 256, 2], P('track'), may hold values from 0 to 199, as said below
- res_index: int32 [8, 4, 524288], P('track', None, 'pix'), may hold values from -128 to 128, as said below
- res_weight: float32 [8, 4, 524288], P('track', None, 'pix'), may hold values from 0.05 to 1
- coverage: int32 [8, 512, 8], P('track', 'pix'), may hold values 0 or 1
- los: float32 [8, 3], replicated
- north: float32 [512, 1024], P('pix'), may hold values from -6 to 6
Outputs:
- east_up: float32 [2, 512, 1024], P(None, 'pix', 'track')
- strain: float32 [3, 512, 1024], P(None, 'pix', 'track')
The draws below stay inside these ranges and needn't reach their ends.
Inputs may be any that keep to these rules, and one draw needn't show every extreme that they name: `pairs`: each row holds an earlier epoch and a strictly later one. `res_index`: cell index plus offset lies within 0 to 524287.
All inputs are finite; a program needn't handle non-finite values. No bound on the sum of `coherent` or of `coverage` on one device may be relied on, other than what follows from the above.
Results may differ from the reference program's by a relative error of at most 0.0031.
Values may be sent and summed in bfloat16 or wider, within the bound.
A program may use at most 128 MiB of HBM per device.

```python
import jax
import jax.numpy as jnp
from jax import lax

IFGS = 256
EPOCHS = 200
GRD = 8
GCOLS = 1024
HALO = 128
CTILE = 128
MBLK = 128
TRACKS = 8
GROWS = 512
NCELLS = 524288


def draw_pairs(key, part):
    first_key, gap_key = jax.random.split(jax.random.fold_in(key, 11))
    first = jax.random.randint(first_key, (TRACKS, IFGS), 0, EPOCHS - 1)
    spread = jax.random.randint(gap_key, (TRACKS, IFGS), 1, EPOCHS // 4 + 2)
    second = jnp.minimum(first + spread, EPOCHS - 1)
    first = first.at[:, 0].set(0)
    second = jnp.maximum(second, first + 1)
    second = second.at[:, IFGS - 1].set(EPOCHS - 1)
    return jnp.stack([first, second], axis=-1).astype(jnp.int32)


def draw_res_index(key, part):
    offset = jax.random.randint(jax.random.fold_in(key, 23), (TRACKS, 4, NCELLS), -HALO, HALO + 1)
    offset = offset.at[:, 0, HALO].set(-HALO)
    offset = offset.at[:, 1, NCELLS - 1 - HALO].set(HALO)
    cells = jnp.arange(NCELLS, dtype=jnp.int32)
    target = jnp.clip(cells[None, None, :] + offset, 0, NCELLS - 1)
    return (target - cells[None, None, :]).astype(jnp.int32)


def draw_los(key, part):
    keys = jax.random.split(jax.random.fold_in(key, 37), 3)
    signs = jnp.where(jnp.arange(TRACKS) % 2 == 0, 1.0, -1.0).astype(jnp.float32)
    east = signs * jax.random.uniform(keys[0], (TRACKS,), jnp.float32, 0.35, 0.7)
    north_c = jax.random.uniform(keys[1], (TRACKS,), jnp.float32, -0.2, 0.2)
    up_c = jax.random.uniform(keys[2], (TRACKS,), jnp.float32, 0.6, 0.9)
    return jnp.stack([east, north_c, up_c], axis=1).astype(jnp.float32)


def set_ends(entries, own_key, least, largest):
    longest = entries.shape.index(max(entries.shape))
    spots = []
    for shift in (0, 1):
        where = [jax.random.randint(jax.random.fold_in(own_key, axis), (), 0, length) for axis, length in enumerate(entries.shape)]
        where[longest] = (where[longest] + shift) % entries.shape[longest]
        spots.append(tuple(where))
    return entries.at[spots[0]].set(least).at[spots[1]].set(largest)


def levels(stream_key, shape, cuts, low, largest):
    gain, own = 1.0, jax.random.fold_in(stream_key, 6)
    for position, shards_of in cuts:
        steps = jnp.exp(jax.random.uniform(jax.random.fold_in(own, position), (shards_of,), jnp.float32, low / len(cuts), largest / len(cuts)))
        gain = gain * jnp.repeat(steps, shape[position] // shards_of).reshape([-1 if axis == position else 1 for axis in range(len(shape))])
    return gain


def scatter_about(stream_key, shape, scale, reach, cuts=(), kind=jnp.bfloat16):
    drawn = scale * jax.random.normal(stream_key, shape, jnp.float32)
    if cuts:
        drawn = drawn * levels(stream_key, shape, cuts, -0.22, 0.18)
    return jnp.clip(drawn, -reach, reach).astype(kind)


def setup_inputs(seed: int = 0) -> dict:
    seeds = jax.random.split(jax.random.key(seed), 9)
    phases = scatter_about(seeds[0], (TRACKS, IFGS, NCELLS), 3.0, 15.0, ((0, 8), (1, 64)))
    coherent = set_ends((jax.random.randint(seeds[1], (TRACKS, IFGS, NCELLS // MBLK), 0, 4) < 3).astype(jnp.int32), jax.random.fold_in(seeds[1], 1), 0, 1)
    pairs = draw_pairs(jax.random.fold_in(seeds[8], 71), 0)
    res_index = draw_res_index(jax.random.fold_in(seeds[8], 71), 0)
    res_weight = jnp.clip(0.05 + 0.95 * jax.random.uniform(seeds[4], (TRACKS, 4, NCELLS), jnp.float32) ** levels(seeds[4], (TRACKS, 4, NCELLS), ((0, 8), (2, 64)), -0.2, 0.2), 0.05, 1.0)
    coverage = set_ends((jax.random.randint(seeds[5], (TRACKS, GROWS, GCOLS // CTILE), 0, 8) < 5).astype(jnp.int32), jax.random.fold_in(seeds[5], 1), 0, 1)
    los = draw_los(jax.random.fold_in(seeds[8], 71), 0)
    north = scatter_about(seeds[7], (GROWS, GCOLS), 1.0, 6.0, ((0, 64),), jnp.float32)
    return dict(phases=phases, coherent=coherent, pairs=pairs, res_index=res_index, res_weight=res_weight, coverage=coverage, los=los, north=north)


prior_var = 0.1
ridge_term = 0.5

def setup_track(pair_rows):
    epochs = jnp.arange(EPOCHS, dtype=jnp.int32)
    design = (epochs[None, :] == pair_rows[:, 1:2]).astype(jnp.float32) - (epochs[None, :] == pair_rows[:, 0:1]).astype(jnp.float32)
    normal = jnp.dot(design.T.astype(jnp.float32), design.astype(jnp.float32), precision=lax.Precision.HIGHEST, preferred_element_type=jnp.float32) + jnp.eye(EPOCHS, dtype=jnp.float32)
    factor = jnp.linalg.cholesky(normal)
    pseudo = jax.scipy.linalg.cho_solve((factor, True), design.T)
    centred = jnp.arange(EPOCHS).astype(jnp.float32) - (EPOCHS - 1) / 2.0
    slope = centred * (EPOCHS - 1) / jnp.sum(centred * centred)
    return (design, pseudo.astype(jnp.bfloat16), slope)

def invert_block(stack, design, pseudo_bf, slope):
    series = jnp.dot(pseudo_bf.astype(jnp.float32), stack.astype(jnp.float32), preferred_element_type=jnp.float32)
    velocity = jnp.dot(slope.astype(jnp.float32), series.astype(jnp.float32), precision=lax.Precision.HIGHEST, preferred_element_type=jnp.float32)
    fitted = jnp.dot(design.astype(jnp.bfloat16).astype(jnp.float32), series.astype(jnp.bfloat16).astype(jnp.float32), preferred_element_type=jnp.float32)
    misfit = stack.astype(jnp.float32) - fitted
    variance = jnp.sum(misfit * misfit, axis=0) / IFGS
    return jnp.stack([velocity, variance])

def solve_cells(vals, cover, north_part, los):
    east_c = los[:, 0][:, None, None]
    north_c = los[:, 1][:, None, None]
    up_c = los[:, 2][:, None, None]
    weight = cover / (vals[1] + prior_var)
    target = vals[0] - north_c * north_part[None]
    a11 = jnp.sum(weight * east_c * east_c, axis=0) + ridge_term
    a12 = jnp.sum(weight * east_c * up_c, axis=0)
    a22 = jnp.sum(weight * up_c * up_c, axis=0) + ridge_term
    b1 = jnp.sum(weight * east_c * target, axis=0)
    b2 = jnp.sum(weight * up_c * target, axis=0)
    determ = a11 * a22 - a12 * a12
    return ((a22 * b1 - a12 * b2) / determ, (a11 * b2 - a12 * b1) / determ)

def stencil(padded):
    east_p = padded[0]
    north_p = padded[1]
    exx = (east_p[1:-1, 2:] - east_p[1:-1, :-2]) / 2.0
    eyy = (north_p[2:, 1:-1] - north_p[:-2, 1:-1]) / 2.0
    exy = (east_p[2:, 1:-1] - east_p[:-2, 1:-1] + north_p[1:-1, 2:] - north_p[1:-1, :-2]) / 4.0
    return jnp.stack([exx, eyy, exy])

def one_track(packed):
    phase_t, flag_t, pair_t, offset_t, weight_t, cover_t = packed
    design, pseudo_bf, slope = setup_track(pair_t)
    blocked = phase_t.reshape(IFGS, NCELLS // MBLK, MBLK)
    masked = jnp.where(flag_t[:, :, None] == 1, blocked, jnp.zeros((), jnp.bfloat16)).reshape(IFGS, NCELLS)
    width = GRD * GCOLS
    pieces = masked.reshape(IFGS, NCELLS // width, width).transpose(1, 0, 2)
    fields = lax.map(lambda piece: invert_block(piece, design, pseudo_bf, slope), pieces)
    fields = fields.transpose(1, 0, 2).reshape(2, NCELLS)
    padded = jnp.pad(fields, ((0, 0), (HALO, HALO)))
    cells = jnp.arange(NCELLS, dtype=jnp.int32)
    picked = padded[:, (cells[None, :] + offset_t + HALO).astype(jnp.int32)]
    grid = jnp.sum(picked * weight_t[None], axis=1) / jnp.sum(weight_t, axis=0)
    tiles = GCOLS // CTILE
    cover = jnp.broadcast_to(cover_t.astype(jnp.float32)[:, :, None], (GROWS, tiles, CTILE)).reshape(GROWS, GCOLS)
    return (grid.reshape(2, GROWS, GCOLS), cover)

def reference(phases, coherent, pairs, res_index, res_weight, coverage, los, north):
    grids, covers = lax.map(one_track, (phases, coherent, pairs, res_index, res_weight, coverage))
    vals = grids.transpose(1, 0, 2, 3)
    east, up = solve_cells(vals, covers, north, los)
    padded = jnp.pad(jnp.stack([east, north]), ((0, 0), (1, 1), (1, 1)))
    return (jnp.stack([east, up]), stencil(padded))
```

```python
import jax
import jax.numpy as jnp
from jax import lax
from jax.experimental import pallas as pl
from jax.experimental.pallas import tpu as pltpu
from jax.sharding import PartitionSpec as P

IFGS = 256
EPOCHS = 200
GRD = 8
GCOLS = 1024
LANES = 128
TILES = GCOLS // LANES
PIX = 64
TRACKS = 8
LOCAL = IFGS // PIX
KPAD = 256

prior_var = 0.1
ridge_term = 0.5

MESH = pl.DeviceIdType.MESH
F32 = jnp.float32
BF16 = jnp.bfloat16
HIGHEST = lax.Precision.HIGHEST


def iota(shape, dim):
    return lax.broadcasted_iota(jnp.int32, shape, dim)


def setup(pairs, normal, weights, design):
    epoch = iota((KPAD, IFGS), 0)
    design_t = (epoch == pairs[1:2, :]).astype(F32) - (epoch == pairs[0:1, :]).astype(F32)
    design[...] = design_t.T.astype(BF16)
    gram = lax.dot_general(
        design_t.astype(BF16), design_t.astype(BF16), (((1,), (1,)), ((), ())), preferred_element_type=F32
    )
    normal[...] = gram + (iota((KPAD, KPAD), 0) == iota((KPAD, KPAD), 1)).astype(F32)

    def eliminate(k, carry):
        row = normal[pl.ds(k, 1), :]
        here = iota((1, KPAD), 1) == k
        inverse = 1.0 / jnp.sum(jnp.where(here, row, 0.0), axis=1, keepdims=True)
        scaled = jnp.where(here, inverse, row * inverse)
        block = normal[0:EPOCHS, :]
        at_k = iota((EPOCHS, KPAD), 1) == k
        column = jnp.sum(jnp.where(at_k, block, 0.0), axis=1, keepdims=True)
        normal[0:EPOCHS, :] = jnp.where(at_k, 0.0, block) - column * scaled
        normal[pl.ds(k, 1), :] = scaled
        return carry

    lax.fori_loop(0, EPOCHS, eliminate, 0)
    pseudo = jnp.dot(normal[...], design_t, precision=HIGHEST, preferred_element_type=F32)
    pseudo = jnp.where(iota((KPAD, IFGS), 0) < EPOCHS, pseudo, 0.0).astype(BF16).astype(F32)
    centred = iota((KPAD, 1), 0).astype(F32) - (EPOCHS - 1) / 2.0
    total = EPOCHS * (EPOCHS * EPOCHS - 1) / 12.0
    slope = centred * (EPOCHS - 1) / total
    rate = jnp.sum(slope * pseudo, axis=0, keepdims=True)
    high = rate.astype(BF16).astype(F32)
    middle = (rate - high).astype(BF16).astype(F32)
    low = rate - high - middle
    row = iota((KPAD, IFGS), 0)
    full = jnp.where(row == EPOCHS, high, pseudo)
    full = jnp.where(row == EPOCHS + 1, middle, full)
    full = jnp.where(row == EPOCHS + 2, low, full)
    weights[...] = full.astype(BF16)


def kernel(
    phases, coherent_h, pairs_h, index_h, weight_h, cover_h, los_h, north_h,
    east_up, strain,
    sent, held, coherent, pairs, index, weight, cover, los, north,
    normal, weights, design, stack, rates, errors, offsets, shares, edge_out, edge_in,
    north_own, north_in, part_out, part_in, east_own, east_in,
    load_sem, small_sem, own_sem, send_sem, recv_sem, side_send, side_recv, part_send, part_recv,
):
    me = lax.axis_index("pix")
    track = lax.axis_index("track")
    after, before = lax.rem(me + 1, PIX), lax.rem(me + PIX - 1, PIX)
    right, left = lax.rem(track + 1, TRACKS), lax.rem(track + TRACKS - 1, TRACKS)

    def row_of(step):
        return lax.rem(GRD - step, GRD)

    def load(step):
        part = pl.ds(row_of(step) * TILES, TILES)
        return pltpu.make_async_copy(phases.at[:, part], sent.at[:, part], load_sem.at[step])

    small = [
        pltpu.make_async_copy(source, target, small_sem.at[i])
        for i, (source, target) in enumerate(
            (
                (coherent_h, coherent), (pairs_h, pairs), (index_h, index), (weight_h, weight),
                (cover_h, cover), (los_h, los), (north_h, north),
            )
        )
    ]
    small[0].start()
    for step in range(GRD):
        load(step).start()
    for copy in small[1:]:
        copy.start()

    barrier = pltpu.get_barrier_semaphore()

    def greet_pix(o, carry):
        pl.semaphore_signal(barrier, inc=1, device_id={"pix": lax.rem(me + o, PIX)}, device_id_type=MESH)
        return carry

    def greet_track(o, carry):
        pl.semaphore_signal(barrier, inc=1, device_id={"track": lax.rem(track + o, TRACKS)}, device_id_type=MESH)
        return carry

    lax.fori_loop(1, PIX, greet_pix, 0)
    lax.fori_loop(1, TRACKS, greet_track, 0)

    def mask(step):
        first = row_of(step) * TILES
        shift = lax.rem(LANES - first, LANES)

        def group(g, carry):
            flags = coherent[:, pl.ds(pl.multiple_of(g * LANES, LANES), LANES)]
            flags = pltpu.roll((flags == 1).astype(F32), shift, 1)
            for h in range(2):
                for t in range(TILES):
                    lane = h * (LANES // 2) + t
                    keep = jnp.broadcast_to(flags[:, lane : lane + 1], (LOCAL, LANES)).astype(BF16)
                    sent[2 * g + h, first + t] = sent[2 * g + h, first + t] * keep
            return carry

        lax.fori_loop(0, PIX // 2, group, 0)

    def ready(step):
        load(step).wait()
        mask(step)

    small[0].wait()
    ready(0)
    pl.semaphore_wait(barrier, PIX - 1 + TRACKS - 1)

    def send(step):
        part = pl.ds(row_of(step) * TILES, TILES)

        def to_peer(i, carry):
            o = PIX - 1 - i
            half = (o + 1) // 2
            peer = lax.rem(me + half + (o % 2) * (PIX - 2 * half), PIX)
            pltpu.make_async_remote_copy(
                src_ref=sent.at[peer, part],
                dst_ref=held.at[part, me],
                send_sem=send_sem,
                recv_sem=recv_sem.at[step],
                device_id={"pix": peer},
                device_id_type=MESH,
            ).start()
            return carry

        lax.fori_loop(0, PIX - 1, to_peer, 0)
        pltpu.make_async_copy(sent.at[me, part], held.at[part, me], own_sem.at[step]).start()

    send(0)

    def rest(step, carry):
        ready(step)
        send(step)
        return carry

    lax.fori_loop(1, GRD, rest, 0)
    for copy in small[1:]:
        copy.wait()

    north_own[...] = north[:, pl.ds(pl.multiple_of(track * LANES, LANES), LANES)]

    def side(source, target, slot, where):
        return pltpu.make_async_remote_copy(
            src_ref=source, dst_ref=target, send_sem=side_send.at[slot], recv_sem=side_recv.at[slot],
            device_id=where, device_id_type=MESH,
        )

    north_down = side(north_own, north_in.at[0], 0, {"pix": after})
    north_up = side(north_own, north_in.at[1], 1, {"pix": before})
    north_down.start()
    north_up.start()

    setup(pairs, normal, weights, design)

    for b in range(4):
        for i in range(GRD):
            offsets[b, i : i + 1, :] = index[b : b + 1, i * GCOLS : (i + 1) * GCOLS]
            shares[b, i : i + 1, :] = weight[b : b + 1, i * GCOLS : (i + 1) * GCOLS]

    def invert(step, carry):
        row = row_of(step)
        part = pl.ds(row * TILES, TILES)
        pltpu.make_async_copy(sent.at[me, part], held.at[part, me], own_sem.at[step]).wait()
        others = held.at[part, pl.ds(0, PIX - 1)]
        pltpu.make_async_copy(others, others, recv_sem.at[step]).wait()
        for t in range(TILES):
            stack[:, t * LANES : (t + 1) * LANES] = held[row * TILES + t].reshape(IFGS, LANES)
        series = jnp.dot(weights[...], stack[...], preferred_element_type=F32)
        rates[pl.ds(row, 1), :] = (
            series[EPOCHS : EPOCHS + 1] + series[EPOCHS + 1 : EPOCHS + 2] + series[EPOCHS + 2 : EPOCHS + 3]
        )
        fitted = jnp.dot(design[...], series.astype(BF16), preferred_element_type=F32)
        misfit = stack[...].astype(F32) - fitted
        errors[pl.ds(row, 1), :] = jnp.sum(misfit * misfit, axis=0, keepdims=True) / IFGS
        return carry

    lax.fori_loop(0, 2, invert, 0)
    edge_out[0, 0] = rates[:, GCOLS - LANES :]
    edge_out[0, 1] = errors[:, GCOLS - LANES :]
    edge_out[1, 0] = rates[:, :LANES]
    edge_out[1, 1] = errors[:, :LANES]
    edge_down = side(edge_out.at[0], edge_in.at[0], 2, {"pix": after})
    edge_up = side(edge_out.at[1], edge_in.at[1], 3, {"pix": before})
    edge_down.start()
    edge_up.start()
    lax.fori_loop(2, GRD, invert, 0)
    edge_down.wait()
    edge_up.wait()

    lane = iota((GRD, LANES), 1)
    row = iota((GRD, LANES), 0)
    lane_los = iota((1, TRACKS), 1)
    north_c = jnp.sum(jnp.where(lane_los == track, los[1:2, :], 0.0), axis=1, keepdims=True)
    covered = cover[...].astype(F32)
    for k in range(TILES):
        span = slice(k * LANES, (k + 1) * LANES)
        picked = [jnp.zeros((GRD, LANES), F32)] * 2
        total = jnp.zeros((GRD, LANES), F32)
        tiles = []
        for f, field in enumerate((rates, errors)):
            if k > 0:
                prev = field[:, (k - 1) * LANES : k * LANES]
            else:
                prev = pltpu.roll(field[:, GCOLS - LANES :], 1, 0)
                prev = jnp.where(row == 0, pltpu.roll(edge_in[0, f], 1, 0), prev)
            if k < TILES - 1:
                later = field[:, (k + 1) * LANES : (k + 2) * LANES]
            else:
                later = pltpu.roll(field[:, :LANES], GRD - 1, 0)
                later = jnp.where(row == GRD - 1, pltpu.roll(edge_in[1, f], GRD - 1, 0), later)
            tiles.append((prev, field[:, span], later))
        for b in range(4):
            place = lane + offsets[b, :, span]
            inner = place & (LANES - 1)
            share = shares[b, :, span]
            total = total + share
            for f in range(2):
                options = [jnp.take_along_axis(tile, inner, axis=1) for tile in tiles[f]]
                value = jnp.where(place < 0, options[0], jnp.where(place >= LANES, options[2], options[1]))
                picked[f] = picked[f] + value * share
        part_out[k, 0] = covered[:, k : k + 1] / (picked[1] / total + prior_var)
        part_out[k, 1] = picked[0] / total - north_c * north[:, span]

    def part(o):
        peer = lax.rem(track + o, TRACKS)
        return pltpu.make_async_remote_copy(
            src_ref=part_out.at[peer], dst_ref=part_in.at[track], send_sem=part_send, recv_sem=part_recv,
            device_id={"track": peer}, device_id_type=MESH,
        )

    for o in range(1, TRACKS):
        part(o).start()
    part_in[track] = part_out[track]
    seven = part_in.at[pl.ds(0, TRACKS - 1)]
    pltpu.make_async_copy(seven, seven, part_recv).wait()

    a11 = jnp.full((GRD, LANES), ridge_term, F32)
    a22 = jnp.full((GRD, LANES), ridge_term, F32)
    a12 = jnp.zeros((GRD, LANES), F32)
    b1 = jnp.zeros((GRD, LANES), F32)
    b2 = jnp.zeros((GRD, LANES), F32)
    for t in range(TRACKS):
        w, y = part_in[t, 0], part_in[t, 1]
        e, u = los[0:1, t : t + 1], los[2:3, t : t + 1]
        we, wu = w * e, w * u
        a11, a12, a22 = a11 + we * e, a12 + we * u, a22 + wu * u
        b1, b2 = b1 + we * y, b2 + wu * y
    determ = a11 * a22 - a12 * a12
    east = (a22 * b1 - a12 * b2) / determ
    east_own[...] = east
    sides = [
        side(east_own, east_in.at[0], 4, {"pix": after}),
        side(east_own, east_in.at[1], 5, {"pix": before}),
        side(east_own, east_in.at[2], 6, {"track": right}),
        side(east_own, east_in.at[3], 7, {"track": left}),
    ]
    for copy in sides:
        copy.start()
    east_up[0] = east
    east_up[1] = (a11 * b2 - a12 * b1) / determ

    pix_first, pix_last = me == 0, me == PIX - 1
    north_down.wait()
    north_up.wait()
    mine = north_own[...]
    above, below = pltpu.roll(north_in[0], 1, 0), pltpu.roll(north_in[1], GRD - 1, 0)
    above = jnp.where(pix_first, 0.0, above)
    below = jnp.where(pix_last, 0.0, below)
    north_m = jnp.where(row == 0, above, pltpu.roll(mine, 1, 0))
    north_p = jnp.where(row == GRD - 1, below, pltpu.roll(mine, GRD - 1, 0))
    west = north[:, pl.ds(pl.multiple_of(left * LANES, LANES), LANES)]
    orient = north[:, pl.ds(pl.multiple_of(right * LANES, LANES), LANES)]
    west = jnp.where(track == 0, 0.0, pltpu.roll(west, 1, 1))
    orient = jnp.where(track == TRACKS - 1, 0.0, pltpu.roll(orient, LANES - 1, 1))
    north_l = jnp.where(lane == 0, west, pltpu.roll(mine, 1, 1))
    north_r = jnp.where(lane == LANES - 1, orient, pltpu.roll(mine, LANES - 1, 1))
    strain[1] = (north_p - north_m) / 2.0

    for copy in sides:
        copy.wait()
    above, below = pltpu.roll(east_in[0], 1, 0), pltpu.roll(east_in[1], GRD - 1, 0)
    above = jnp.where(pix_first, 0.0, above)
    below = jnp.where(pix_last, 0.0, below)
    west = jnp.where(track == 0, 0.0, pltpu.roll(east_in[2], 1, 1))
    orient = jnp.where(track == TRACKS - 1, 0.0, pltpu.roll(east_in[3], LANES - 1, 1))
    east_m = jnp.where(row == 0, above, pltpu.roll(east, 1, 0))
    east_p = jnp.where(row == GRD - 1, below, pltpu.roll(east, GRD - 1, 0))
    east_l = jnp.where(lane == 0, west, pltpu.roll(east, 1, 1))
    east_r = jnp.where(lane == LANES - 1, orient, pltpu.roll(east, LANES - 1, 1))
    strain[0] = (east_r - east_l) / 2.0
    strain[2] = (east_p - east_m + north_r - north_l) / 4.0

    pltpu.make_async_copy(seven, seven, part_send).wait()
    others = sent.at[pl.ds(0, PIX - 1)]
    pltpu.make_async_copy(others, others, send_sem).wait()


def per_device(phases, coherent, pairs, res_index, res_weight, coverage, los, north):
    tiles = phases.shape[2] // PIX // LANES
    stack = phases[0].reshape(LOCAL, PIX, tiles, LANES).transpose(1, 2, 0, 3)
    hbm = pl.BlockSpec(memory_space=pl.ANY)
    vmem = pl.BlockSpec(memory_space=pltpu.VMEM)
    dma = pltpu.SemaphoreType.DMA
    width = GRD * GCOLS
    return pl.pallas_call(
        kernel,
        out_shape=(
            jax.ShapeDtypeStruct((2, GRD, LANES), F32),
            jax.ShapeDtypeStruct((3, GRD, LANES), F32),
        ),
        in_specs=[hbm] * 8,
        out_specs=(vmem, vmem),
        scratch_shapes=[
            pltpu.VMEM((PIX, tiles, LOCAL, LANES), BF16),
            pltpu.VMEM((tiles, PIX, LOCAL, LANES), BF16),
            pltpu.VMEM(coherent.shape[1:], jnp.int32),
            pltpu.VMEM((2, IFGS), jnp.int32),
            pltpu.VMEM((4, width), jnp.int32),
            pltpu.VMEM((4, width), F32),
            pltpu.VMEM((GRD, TILES), jnp.int32),
            pltpu.VMEM((3, TRACKS), F32),
            pltpu.VMEM((GRD, GCOLS), F32),
            pltpu.VMEM((KPAD, KPAD), F32),
            pltpu.VMEM((KPAD, IFGS), BF16),
            pltpu.VMEM((IFGS, KPAD), BF16),
            pltpu.VMEM((IFGS, GCOLS), BF16),
            pltpu.VMEM((GRD, GCOLS), F32),
            pltpu.VMEM((GRD, GCOLS), F32),
            pltpu.VMEM((4, GRD, GCOLS), jnp.int32),
            pltpu.VMEM((4, GRD, GCOLS), F32),
            pltpu.VMEM((2, 2, GRD, LANES), F32),
            pltpu.VMEM((2, 2, GRD, LANES), F32),
            pltpu.VMEM((GRD, LANES), F32),
            pltpu.VMEM((2, GRD, LANES), F32),
            pltpu.VMEM((TRACKS, 2, GRD, LANES), F32),
            pltpu.VMEM((TRACKS, 2, GRD, LANES), F32),
            pltpu.VMEM((GRD, LANES), F32),
            pltpu.VMEM((4, GRD, LANES), F32),
            dma((GRD,)),
            dma((7,)),
            dma((GRD,)),
            dma(()),
            dma((GRD,)),
            dma((8,)),
            dma((8,)),
            dma(()),
            dma(()),
        ],
        compiler_params=pltpu.CompilerParams(collective_id=0, has_side_effects=True),
    )(stack, coherent[0], pairs[0].T, res_index[0], res_weight[0], coverage[0], los.T, north)


def solution(mesh):
    in_specs = (
        P("track", "pix", None),
        P("track", "pix", None),
        P("track", None, None),
        P("track", None, "pix"),
        P("track", None, "pix"),
        P("track", "pix", None),
        P(),
        P("pix", None),
    )
    out_specs = (P(None, "pix", "track"), P(None, "pix", "track"))
    return jax.shard_map(
        per_device, mesh=mesh, in_specs=in_specs, out_specs=out_specs, check_vma=False
    )
```

```python
import jax
import jax.numpy as jnp
from jax import lax
from jax.experimental import pallas as pl
from jax.experimental.pallas import tpu as pltpu
from jax.sharding import PartitionSpec as P

IFGS = 256
EPOCHS = 200
GRD = 8
GCOLS = 1024
LANES = 128
TILES = GCOLS // LANES
PIX = 64
TRACKS = 8
RING = 4
RINGS = PIX // RING
REACH = 4
EARLY = 2
LOCAL = IFGS // PIX
KPAD = 256
BATCH = 4

prior_var = 0.1
ridge_term = 0.5

MESH = pl.DeviceIdType.MESH
F32 = jnp.float32
BF16 = jnp.bfloat16
HIGHEST = lax.Precision.HIGHEST


def iota(shape, dim):
    return lax.broadcasted_iota(jnp.int32, shape, dim)


def setup(pairs, normal, weights, design):
    epoch = iota((KPAD, IFGS), 0)
    design_t = (epoch == pairs[1:2, :]).astype(F32) - (epoch == pairs[0:1, :]).astype(F32)
    design[...] = design_t.T.astype(BF16)
    gram = lax.dot_general(
        design_t.astype(BF16), design_t.astype(BF16), (((1,), (1,)), ((), ())), preferred_element_type=F32
    )
    normal[...] = gram + (iota((KPAD, KPAD), 0) == iota((KPAD, KPAD), 1)).astype(F32)

    def eliminate(k, carry):
        row = normal[pl.ds(k, 1), :]
        here = iota((1, KPAD), 1) == k
        inverse = 1.0 / jnp.sum(jnp.where(here, row, 0.0), axis=1, keepdims=True)
        scaled = jnp.where(here, inverse, row * inverse)
        block = normal[0:EPOCHS, :]
        at_k = iota((EPOCHS, KPAD), 1) == k
        column = jnp.sum(jnp.where(at_k, block, 0.0), axis=1, keepdims=True)
        normal[0:EPOCHS, :] = jnp.where(at_k, 0.0, block) - column * scaled
        normal[pl.ds(k, 1), :] = scaled
        return carry

    lax.fori_loop(0, EPOCHS, eliminate, 0)
    pseudo = jnp.dot(normal[...], design_t, precision=HIGHEST, preferred_element_type=F32)
    pseudo = jnp.where(iota((KPAD, IFGS), 0) < EPOCHS, pseudo, 0.0).astype(BF16).astype(F32)
    centred = iota((KPAD, 1), 0).astype(F32) - (EPOCHS - 1) / 2.0
    total = EPOCHS * (EPOCHS * EPOCHS - 1) / 12.0
    slope = centred * (EPOCHS - 1) / total
    rate = jnp.sum(slope * pseudo, axis=0, keepdims=True)
    high = rate.astype(BF16).astype(F32)
    middle = (rate - high).astype(BF16).astype(F32)
    low = rate - high - middle
    row = iota((KPAD, IFGS), 0)
    full = jnp.where(row == EPOCHS, high, pseudo)
    full = jnp.where(row == EPOCHS + 1, middle, full)
    full = jnp.where(row == EPOCHS + 2, low, full)
    weights[...] = full.astype(BF16)


def kernel(
    phases, coherent_h, pairs_h, index_h, weight_h, cover_h, los_h, north_h,
    result,
    sent, held, coherent, pairs, index, weight, cover, los, north,
    normal, weights, design, stack, rates, errors, offsets, shares, covered, edge_out, edge_in,
    north_own, north_in, part_out, part_in, east_own, east_in,
    load_sem, small_sem, own_sem, send_sem, recv_sem, side_send, side_recv, part_send, part_recv, relay_sem,
):
    me = lax.axis_index("pix")
    track = lax.axis_index("track")
    after, before = lax.rem(me + 1, PIX), lax.rem(me + PIX - 1, PIX)
    right, left = lax.rem(track + 1, TRACKS), lax.rem(track + TRACKS - 1, TRACKS)

    def tile_of(step):
        return lax.rem(step + TILES - 1, TILES)

    def load(step):
        k = tile_of(step)
        return pltpu.make_async_copy(phases.at[:, :, k], sent.at[k], load_sem.at[step])

    small = [
        pltpu.make_async_copy(source, target, small_sem.at[i])
        for i, (source, target) in enumerate(
            (
                (coherent_h, coherent), (pairs_h, pairs), (index_h, index), (weight_h, weight),
                (cover_h, cover), (los_h, los), (north_h, north),
            )
        )
    ]
    small[0].start()
    for step in range(TILES):
        load(step).start()
    for copy in small[1:]:
        copy.start()

    barrier = pltpu.get_barrier_semaphore()

    def at(down, over):
        return lax.rem(me // RING + down, RINGS) * RING + lax.rem(me % RING + over, RING)

    def near(i):
        n = 2 * REACH - 1 - i // RING
        half = n // 2 + 1
        return at(half + (1 - n % 2) * (RINGS - 2 * half), i % RING)

    def far(i):
        n = RINGS - 2 * REACH - 2 - i // RING
        half = REACH + 1 + n // 2
        return at(half + (1 - n % 2) * (RINGS - 2 * half), i % RING)

    def greet(peer):
        pl.semaphore_signal(barrier, inc=1, device_id={"pix": peer}, device_id_type=MESH)

    def greet_near(i, carry):
        greet(near(i))
        return carry

    def greet_track(o, carry):
        pl.semaphore_signal(barrier, inc=1, device_id={"track": lax.rem(track + o, TRACKS)}, device_id_type=MESH)
        return carry

    lax.fori_loop(0, 2 * REACH * RING, greet_near, 0)
    for over in range(1, RING):
        greet(at(0, over))
    lax.fori_loop(1, TRACKS, greet_track, 0)

    def mask(k, shift, groups):
        kept = []
        for g in groups:
            flags = coherent[:, pl.ds(pl.multiple_of(g * LANES, LANES), LANES)]
            flags = pltpu.roll((flags == 1).astype(F32), shift, 1)
            for h in range(2):
                for i in range(GRD):
                    lane = h * (LANES // 2) + i * TILES
                    keep = jnp.broadcast_to(flags[:, lane : lane + 1], (LOCAL, LANES)).astype(BF16)
                    kept.append((2 * g + h, i, sent[k, 2 * g + h, i] * keep))
        for peer, i, value in kept:
            sent[k, peer, i] = value

    def send(step, k, peer):
        pltpu.make_async_remote_copy(
            src_ref=sent.at[k, peer],
            dst_ref=held.at[k, :, me],
            send_sem=send_sem,
            recv_sem=recv_sem.at[step],
            device_id={"pix": peer},
            device_id_type=MESH,
        ).start()

    def own(step, k):
        return pltpu.make_async_copy(sent.at[k, me], held.at[k, :, me], own_sem.at[step])

    def ready(step):
        load(step).wait()
        k = tile_of(step)
        shift = lax.rem(LANES - k, LANES)

        def group(g, carry):
            mask(k, shift, [BATCH * g + m for m in range(BATCH)])
            return carry

        lax.fori_loop(0, PIX // 2 // BATCH, group, 0)

    def send_near(step):
        k = tile_of(step)

        def to_peer(i, carry):
            send(step, k, near(i))
            return carry

        lax.fori_loop(0, 2 * REACH * RING, to_peer, 0)
        for over in range(1, RING):
            send(step, k, at(0, over))

    def send_far(step):
        k = tile_of(step)

        def to_peer(i, carry):
            send(step, k, far(i))
            return carry

        lax.fori_loop(0, (RINGS - 2 * REACH - 1) * RING, to_peer, 0)
        own(step, k).start()

    def rest(step, carry):
        ready(step)
        send_far(step)
        send_near(step)
        return carry

    small[0].wait()
    ready(0)
    pl.semaphore_wait(barrier, (2 * REACH + 1) * RING - 1 + TRACKS - 1)
    for down in (REACH, RINGS - REACH):
        pl.semaphore_signal(relay_sem, inc=1, device_id={"pix": at(down, 0)}, device_id_type=MESH)
    for step in range(EARLY):
        if step:
            ready(step)
        send_near(step)
    pl.semaphore_wait(relay_sem, 2)
    for step in range(EARLY):
        send_far(step)
    lax.fori_loop(EARLY, TILES, rest, 0)
    for copy in small[1:]:
        copy.wait()

    north_own[...] = north[:, pl.ds(pl.multiple_of(track * LANES, LANES), LANES)]

    def side(source, target, slot, where):
        return pltpu.make_async_remote_copy(
            src_ref=source, dst_ref=target, send_sem=side_send.at[slot], recv_sem=side_recv.at[slot],
            device_id=where, device_id_type=MESH,
        )

    north_down = side(north_own, north_in.at[0], 0, {"pix": after})
    north_up = side(north_own, north_in.at[1], 1, {"pix": before})
    north_down.start()
    north_up.start()

    setup(pairs, normal, weights, design)

    lane = iota((GRD, LANES), 1)
    row = iota((GRD, LANES), 0)
    flags = cover[...].astype(F32)
    for k in range(TILES):
        covered[k] = jnp.broadcast_to(flags[:, k : k + 1], (GRD, LANES))
        for b in range(4):
            for i in range(GRD):
                begin = i * GCOLS + k * LANES
                offsets[k, b, i : i + 1, :] = index[b : b + 1, begin : begin + LANES] + lane[:1]
                shares[k, b, i : i + 1, :] = weight[b : b + 1, begin : begin + LANES]
    lane_los = iota((1, TRACKS), 1)
    north_c = jnp.sum(jnp.where(lane_los == track, los[1:2, :], 0.0), axis=1, keepdims=True)

    def invert(step):
        k = tile_of(step)
        own(step, k).wait()
        others = held.at[k, :, pl.ds(0, PIX - 1)]
        pltpu.make_async_copy(others, others, recv_sem.at[step]).wait()
        for i in range(GRD):
            stack[:, i * LANES : (i + 1) * LANES] = held[k, i].reshape(IFGS, LANES)
        series = jnp.dot(weights[...], stack[...], preferred_element_type=F32)
        rate = series[EPOCHS : EPOCHS + 1] + series[EPOCHS + 1 : EPOCHS + 2] + series[EPOCHS + 2 : EPOCHS + 3]
        fitted = jnp.dot(design[...], series.astype(BF16), preferred_element_type=F32)
        misfit = stack[...].astype(F32) - fitted
        error = jnp.sum(misfit * misfit, axis=0, keepdims=True) / IFGS
        for i in range(GRD):
            rates[k + 1, i : i + 1, :] = rate[:, i * LANES : (i + 1) * LANES]
            errors[k + 1, i : i + 1, :] = error[:, i * LANES : (i + 1) * LANES]

    def part(k):
        return pltpu.make_async_remote_copy(
            src_ref=part_out.at[k], dst_ref=part_in.at[track], send_sem=part_send, recv_sem=part_recv,
            device_id={"track": k}, device_id_type=MESH,
        )

    def resample(k):
        tiles = [[field[k + n] for n in range(3)] for field in (rates, errors)]
        picked = [jnp.zeros((GRD, LANES), F32)] * 2
        total = jnp.zeros((GRD, LANES), F32)
        for b in range(4):
            place = offsets[k, b]
            inner = place & (LANES - 1)
            share = shares[k, b]
            total = total + share
            for f in range(2):
                options = [jnp.take_along_axis(tile, inner, axis=1) for tile in tiles[f]]
                value = jnp.where(place < 0, options[0], jnp.where(place >= LANES, options[2], options[1]))
                picked[f] = picked[f] + value * share
        part_out[k, 0] = covered[k] / (picked[1] / total + prior_var)
        part_out[k, 1] = picked[0] / total - north_c * north[:, pl.ds(pl.multiple_of(k * LANES, LANES), LANES)]

        @pl.when(k != track)
        def _():
            part(k).start()

    invert(0)
    invert(1)
    edge_out[0, 0] = rates[TILES]
    edge_out[0, 1] = errors[TILES]
    edge_out[1, 0] = rates[1]
    edge_out[1, 1] = errors[1]
    edge_down = side(edge_out.at[0], edge_in.at[0], 2, {"pix": after})
    edge_up = side(edge_out.at[1], edge_in.at[1], 3, {"pix": before})
    edge_down.start()
    edge_up.start()
    invert(2)
    edge_down.wait()
    edge_up.wait()
    for f, field in enumerate((rates, errors)):
        field[0] = jnp.where(row == 0, pltpu.roll(edge_in[0, f], 1, 0), pltpu.roll(field[TILES], 1, 0))
        field[TILES + 1] = jnp.where(
            row == GRD - 1, pltpu.roll(edge_in[1, f], GRD - 1, 0), pltpu.roll(field[1], GRD - 1, 0)
        )
    resample(0)

    def advance(step, carry):
        invert(step)
        resample(step - 2)
        return carry

    lax.fori_loop(3, TILES, advance, 0)
    resample(TILES - 2)
    resample(TILES - 1)
    part_in[track] = part_out[track]
    seven = part_in.at[pl.ds(0, TRACKS - 1)]
    pltpu.make_async_copy(seven, seven, part_recv).wait()

    a11 = jnp.full((GRD, LANES), ridge_term, F32)
    a22 = jnp.full((GRD, LANES), ridge_term, F32)
    a12 = jnp.zeros((GRD, LANES), F32)
    b1 = jnp.zeros((GRD, LANES), F32)
    b2 = jnp.zeros((GRD, LANES), F32)
    for t in range(TRACKS):
        w, y = part_in[t, 0], part_in[t, 1]
        e, u = los[0:1, t : t + 1], los[2:3, t : t + 1]
        we, wu = w * e, w * u
        a11, a12, a22 = a11 + we * e, a12 + we * u, a22 + wu * u
        b1, b2 = b1 + we * y, b2 + wu * y
    determ = a11 * a22 - a12 * a12
    east = (a22 * b1 - a12 * b2) / determ
    east_own[...] = east
    sides = [
        side(east_own, east_in.at[0], 4, {"pix": after}),
        side(east_own, east_in.at[1], 5, {"pix": before}),
        side(east_own, east_in.at[2], 6, {"track": right}),
        side(east_own, east_in.at[3], 7, {"track": left}),
    ]
    for copy in sides:
        copy.start()
    result[0] = east
    result[1] = (a11 * b2 - a12 * b1) / determ

    pix_first, pix_last = me == 0, me == PIX - 1
    north_down.wait()
    north_up.wait()
    mine = north_own[...]
    above, below = pltpu.roll(north_in[0], 1, 0), pltpu.roll(north_in[1], GRD - 1, 0)
    above = jnp.where(pix_first, 0.0, above)
    below = jnp.where(pix_last, 0.0, below)
    north_m = jnp.where(row == 0, above, pltpu.roll(mine, 1, 0))
    north_p = jnp.where(row == GRD - 1, below, pltpu.roll(mine, GRD - 1, 0))
    west = north[:, pl.ds(pl.multiple_of(left * LANES, LANES), LANES)]
    orient = north[:, pl.ds(pl.multiple_of(right * LANES, LANES), LANES)]
    west = jnp.where(track == 0, 0.0, pltpu.roll(west, 1, 1))
    orient = jnp.where(track == TRACKS - 1, 0.0, pltpu.roll(orient, LANES - 1, 1))
    north_l = jnp.where(lane == 0, west, pltpu.roll(mine, 1, 1))
    north_r = jnp.where(lane == LANES - 1, orient, pltpu.roll(mine, LANES - 1, 1))
    result[3] = (north_p - north_m) / 2.0

    for copy in sides:
        copy.wait()
    above, below = pltpu.roll(east_in[0], 1, 0), pltpu.roll(east_in[1], GRD - 1, 0)
    above = jnp.where(pix_first, 0.0, above)
    below = jnp.where(pix_last, 0.0, below)
    west = jnp.where(track == 0, 0.0, pltpu.roll(east_in[2], 1, 1))
    orient = jnp.where(track == TRACKS - 1, 0.0, pltpu.roll(east_in[3], LANES - 1, 1))
    east_m = jnp.where(row == 0, above, pltpu.roll(east, 1, 0))
    east_p = jnp.where(row == GRD - 1, below, pltpu.roll(east, GRD - 1, 0))
    east_l = jnp.where(lane == 0, west, pltpu.roll(east, 1, 1))
    east_r = jnp.where(lane == LANES - 1, orient, pltpu.roll(east, LANES - 1, 1))
    result[2] = (east_r - east_l) / 2.0
    result[4] = (east_p - east_m + north_r - north_l) / 4.0

    pltpu.make_async_copy(seven, seven, part_send).wait()
    others = sent.at[:, pl.ds(0, PIX - 1)]
    pltpu.make_async_copy(others, others, send_sem).wait()


def deliver(result, east_up, strain):
    east_up[...] = result[0:2]
    strain[...] = result[2:5]


def per_device(phases, coherent, pairs, res_index, res_weight, coverage, los, north):
    stack = phases[0].reshape(LOCAL, PIX, GRD, TILES, LANES).transpose(1, 2, 3, 0, 4)
    hbm = pl.BlockSpec(memory_space=pl.ANY)
    vmem = pl.BlockSpec(memory_space=pltpu.VMEM)
    dma = pltpu.SemaphoreType.DMA
    width = GRD * GCOLS
    tile = (GRD, LANES)
    result = pl.pallas_call(
        kernel,
        out_shape=jax.ShapeDtypeStruct((5, *tile), F32),
        in_specs=[hbm] * 8,
        out_specs=vmem,
        scratch_shapes=[
            pltpu.VMEM((TILES, PIX, GRD, LOCAL, LANES), BF16),
            pltpu.VMEM((TILES, GRD, PIX, LOCAL, LANES), BF16),
            pltpu.VMEM(coherent.shape[1:], jnp.int32),
            pltpu.VMEM((2, IFGS), jnp.int32),
            pltpu.VMEM((4, width), jnp.int32),
            pltpu.VMEM((4, width), F32),
            pltpu.VMEM((GRD, TILES), jnp.int32),
            pltpu.VMEM((3, TRACKS), F32),
            pltpu.VMEM((GRD, GCOLS), F32),
            pltpu.VMEM((KPAD, KPAD), F32),
            pltpu.VMEM((KPAD, IFGS), BF16),
            pltpu.VMEM((IFGS, KPAD), BF16),
            pltpu.VMEM((IFGS, GCOLS), BF16),
            pltpu.VMEM((TILES + 2, *tile), F32),
            pltpu.VMEM((TILES + 2, *tile), F32),
            pltpu.VMEM((TILES, 4, *tile), jnp.int32),
            pltpu.VMEM((TILES, 4, *tile), F32),
            pltpu.VMEM((TILES, *tile), F32),
            pltpu.VMEM((2, 2, *tile), F32),
            pltpu.VMEM((2, 2, *tile), F32),
            pltpu.VMEM(tile, F32),
            pltpu.VMEM((2, *tile), F32),
            pltpu.VMEM((TRACKS, 2, *tile), F32),
            pltpu.VMEM((TRACKS, 2, *tile), F32),
            pltpu.VMEM(tile, F32),
            pltpu.VMEM((4, *tile), F32),
            dma((TILES,)),
            dma((7,)),
            dma((TILES,)),
            dma(()),
            dma((TILES,)),
            dma((8,)),
            dma((8,)),
            dma(()),
            dma(()),
            pltpu.SemaphoreType.REGULAR,
        ],
        compiler_params=pltpu.CompilerParams(collective_id=0, has_side_effects=True),
    )(stack, coherent[0], pairs[0].T, res_index[0], res_weight[0], coverage[0], los.T, north)
    return pl.pallas_call(
        deliver,
        out_shape=(jax.ShapeDtypeStruct((2, *tile), F32), jax.ShapeDtypeStruct((3, *tile), F32)),
        in_specs=[vmem],
        out_specs=(vmem, vmem),
    )(result)


def solution(mesh):
    in_specs = (
        P("track", "pix", None),
        P("track", "pix", None),
        P("track", None, None),
        P("track", None, "pix"),
        P("track", None, "pix"),
        P("track", "pix", None),
        P(),
        P("pix", None),
    )
    out_specs = (P(None, "pix", "track"), P(None, "pix", "track"))
    return jax.shard_map(
        per_device, mesh=mesh, in_specs=in_specs, out_specs=out_specs, check_vma=False
    )
```

```python
import jax
import jax.numpy as jnp
from jax import lax
from jax.experimental import pallas as pl
from jax.experimental.pallas import tpu as pltpu
from jax.sharding import PartitionSpec as P

IFGS = 256
EPOCHS = 200
GRD = 8
GCOLS = 1024
LANES = 128
TILES = GCOLS // LANES
PIX = 64
TRACKS = 8
RING = 4
RINGS = PIX // RING
REACH = 4
EARLY = 2
LOCAL = IFGS // PIX
KPAD = 256
BATCH = 4

prior_var = 0.1
ridge_term = 0.5

MESH = pl.DeviceIdType.MESH
F32 = jnp.float32
BF16 = jnp.bfloat16
HIGHEST = lax.Precision.HIGHEST


def iota(shape, dim):
    return lax.broadcasted_iota(jnp.int32, shape, dim)


def setup(pairs, normal, weights, design):
    epoch = iota((KPAD, IFGS), 0)
    design_t = (epoch == pairs[1:2, :]).astype(F32) - (epoch == pairs[0:1, :]).astype(F32)
    design[...] = design_t.T.astype(BF16)
    gram = lax.dot_general(
        design_t.astype(BF16), design_t.astype(BF16), (((1,), (1,)), ((), ())), preferred_element_type=F32
    )
    normal[...] = gram + (iota((KPAD, KPAD), 0) == iota((KPAD, KPAD), 1)).astype(F32)

    def eliminate(k, carry):
        row = normal[pl.ds(k, 1), :]
        here = iota((1, KPAD), 1) == k
        inverse = 1.0 / jnp.sum(jnp.where(here, row, 0.0), axis=1, keepdims=True)
        scaled = jnp.where(here, inverse, row * inverse)
        block = normal[0:EPOCHS, :]
        at_k = iota((EPOCHS, KPAD), 1) == k
        column = jnp.sum(jnp.where(at_k, block, 0.0), axis=1, keepdims=True)
        normal[0:EPOCHS, :] = jnp.where(at_k, 0.0, block) - column * scaled
        normal[pl.ds(k, 1), :] = scaled
        return carry

    lax.fori_loop(0, EPOCHS, eliminate, 0)
    pseudo = jnp.dot(normal[...], design_t, precision=HIGHEST, preferred_element_type=F32)
    pseudo = jnp.where(iota((KPAD, IFGS), 0) < EPOCHS, pseudo, 0.0).astype(BF16).astype(F32)
    centred = iota((KPAD, 1), 0).astype(F32) - (EPOCHS - 1) / 2.0
    total = EPOCHS * (EPOCHS * EPOCHS - 1) / 12.0
    slope = centred * (EPOCHS - 1) / total
    rate = jnp.sum(slope * pseudo, axis=0, keepdims=True)
    high = rate.astype(BF16).astype(F32)
    middle = (rate - high).astype(BF16).astype(F32)
    low = rate - high - middle
    row = iota((KPAD, IFGS), 0)
    full = jnp.where(row == EPOCHS, high, pseudo)
    full = jnp.where(row == EPOCHS + 1, middle, full)
    full = jnp.where(row == EPOCHS + 2, low, full)
    weights[...] = full.astype(BF16)


def kernel(
    phases, coherent_h, pairs_h, index_h, weight_h, cover_h, los_h, north_h,
    result,
    sent, held, coherent, pairs, index, weight, cover, los, north,
    normal, weights, design, stack, rates, errors, offsets, shares, covered, edge_out, edge_in,
    north_own, north_in, part_out, part_in, east_own, east_in,
    load_sem, small_sem, own_sem, send_sem, recv_sem, side_send, side_recv, part_send, part_recv, relay_sem,
):
    me = lax.axis_index("pix")
    track = lax.axis_index("track")
    after, before = lax.rem(me + 1, PIX), lax.rem(me + PIX - 1, PIX)
    right, left = lax.rem(track + 1, TRACKS), lax.rem(track + TRACKS - 1, TRACKS)

    def tile_of(step):
        return lax.rem(step + TILES - 1, TILES)

    def load(step):
        k = tile_of(step)
        return pltpu.make_async_copy(phases.at[:, :, k], sent.at[k], load_sem.at[step])

    small = [
        pltpu.make_async_copy(source, target, small_sem.at[i])
        for i, (source, target) in enumerate(
            (
                (coherent_h, coherent), (pairs_h, pairs), (index_h, index), (weight_h, weight),
                (cover_h, cover), (los_h, los), (north_h, north),
            )
        )
    ]
    small[0].start()
    for step in range(TILES):
        load(step).start()
    for copy in small[1:]:
        copy.start()

    barrier = pltpu.get_barrier_semaphore()

    def at(down, over):
        return lax.rem(me // RING + down, RINGS) * RING + lax.rem(me % RING + over, RING)

    def near(i):
        n = 2 * REACH - 1 - i // RING
        half = n // 2 + 1
        return at(half + (1 - n % 2) * (RINGS - 2 * half), i % RING)

    def far(i):
        n = RINGS - 2 * REACH - 2 - i // RING
        half = REACH + 1 + n // 2
        return at(half + (1 - n % 2) * (RINGS - 2 * half), i % RING)

    def greet(peer):
        pl.semaphore_signal(barrier, inc=1, device_id={"pix": peer}, device_id_type=MESH)

    def greet_near(i, carry):
        greet(near(i))
        return carry

    def greet_track(o, carry):
        pl.semaphore_signal(barrier, inc=1, device_id={"track": lax.rem(track + o, TRACKS)}, device_id_type=MESH)
        return carry

    lax.fori_loop(0, 2 * REACH * RING, greet_near, 0)
    for over in range(1, RING):
        greet(at(0, over))
    lax.fori_loop(1, TRACKS, greet_track, 0)

    def mask(k, shift, groups):
        kept = []
        for g in groups:
            flags = coherent[:, pl.ds(pl.multiple_of(g * LANES, LANES), LANES)]
            flags = pltpu.roll((flags == 1).astype(F32), shift, 1)
            for h in range(2):
                for i in range(GRD):
                    lane = h * (LANES // 2) + i * TILES
                    keep = jnp.broadcast_to(flags[:, lane : lane + 1], (LOCAL, LANES)).astype(BF16)
                    kept.append((2 * g + h, i, sent[k, 2 * g + h, i] * keep))
        for peer, i, value in kept:
            sent[k, peer, i] = value

    def send(step, k, peer):
        pltpu.make_async_remote_copy(
            src_ref=sent.at[k, peer],
            dst_ref=held.at[k, :, me],
            send_sem=send_sem,
            recv_sem=recv_sem.at[step],
            device_id={"pix": peer},
            device_id_type=MESH,
        ).start()

    def own(step, k):
        return pltpu.make_async_copy(sent.at[k, me], held.at[k, :, me], own_sem.at[step])

    def ready(step):
        load(step).wait()
        k = tile_of(step)
        shift = lax.rem(LANES - k, LANES)

        def group(g, carry):
            mask(k, shift, [BATCH * g + m for m in range(BATCH)])
            return carry

        lax.fori_loop(0, PIX // 2 // BATCH, group, 0)

    def send_near(step):
        k = tile_of(step)

        def to_peer(i, carry):
            send(step, k, near(i))
            return carry

        lax.fori_loop(0, 2 * REACH * RING, to_peer, 0)
        for over in range(1, RING):
            send(step, k, at(0, over))

    def send_far(step):
        k = tile_of(step)

        def to_peer(i, carry):
            send(step, k, far(i))
            return carry

        lax.fori_loop(0, (RINGS - 2 * REACH - 1) * RING, to_peer, 0)
        own(step, k).start()

    def rest(step, carry):
        ready(step)
        send_far(step)
        send_near(step)
        return carry

    small[0].wait()
    ready(0)
    pl.semaphore_wait(barrier, (2 * REACH + 1) * RING - 1 + TRACKS - 1)
    for down in (REACH, RINGS - REACH):
        pl.semaphore_signal(relay_sem, inc=1, device_id={"pix": at(down, 0)}, device_id_type=MESH)
    for step in range(EARLY):
        if step:
            ready(step)
        send_near(step)
    pl.semaphore_wait(relay_sem, 2)
    for step in range(EARLY):
        send_far(step)
    lax.fori_loop(EARLY, TILES, rest, 0)
    for copy in small[1:]:
        copy.wait()

    north_own[...] = north[:, pl.ds(pl.multiple_of(track * LANES, LANES), LANES)]

    def side(source, target, slot, where):
        return pltpu.make_async_remote_copy(
            src_ref=source, dst_ref=target, send_sem=side_send.at[slot], recv_sem=side_recv.at[slot],
            device_id=where, device_id_type=MESH,
        )

    north_down = side(north_own, north_in.at[0], 0, {"pix": after})
    north_up = side(north_own, north_in.at[1], 1, {"pix": before})
    north_down.start()
    north_up.start()

    setup(pairs, normal, weights, design)

    lane = iota((GRD, LANES), 1)
    row = iota((GRD, LANES), 0)
    flags = cover[...].astype(F32)
    for k in range(TILES):
        covered[k] = jnp.broadcast_to(flags[:, k : k + 1], (GRD, LANES))
        for b in range(4):
            for i in range(GRD):
                begin = i * GCOLS + k * LANES
                offsets[k, b, i : i + 1, :] = index[b : b + 1, begin : begin + LANES] + lane[:1]
                shares[k, b, i : i + 1, :] = weight[b : b + 1, begin : begin + LANES]
    lane_los = iota((1, TRACKS), 1)
    north_c = jnp.sum(jnp.where(lane_los == track, los[1:2, :], 0.0), axis=1, keepdims=True)

    def invert(step):
        k = tile_of(step)
        own(step, k).wait()
        others = held.at[k, :, pl.ds(0, PIX - 1)]
        pltpu.make_async_copy(others, others, recv_sem.at[step]).wait()
        for i in range(GRD):
            stack[:, i * LANES : (i + 1) * LANES] = held[k, i].reshape(IFGS, LANES)
        series = jnp.dot(weights[...], stack[...], preferred_element_type=F32)
        rate = series[EPOCHS : EPOCHS + 1] + series[EPOCHS + 1 : EPOCHS + 2] + series[EPOCHS + 2 : EPOCHS + 3]
        fitted = jnp.dot(design[...], series.astype(BF16), preferred_element_type=F32)
        misfit = stack[...].astype(F32) - fitted
        error = jnp.sum(misfit * misfit, axis=0, keepdims=True) / IFGS
        for i in range(GRD):
            rates[k + 1, i : i + 1, :] = rate[:, i * LANES : (i + 1) * LANES]
            errors[k + 1, i : i + 1, :] = error[:, i * LANES : (i + 1) * LANES]

    def part(k):
        return pltpu.make_async_remote_copy(
            src_ref=part_out.at[k], dst_ref=part_in.at[track], send_sem=part_send, recv_sem=part_recv,
            device_id={"track": k}, device_id_type=MESH,
        )

    def resampled(k):
        tiles = [[field[k + n] for n in range(3)] for field in (rates, errors)]
        picked = [jnp.zeros((GRD, LANES), F32)] * 2
        total = jnp.zeros((GRD, LANES), F32)
        for b in range(4):
            place = offsets[k, b]
            inner = place & (LANES - 1)
            share = shares[k, b]
            total = total + share
            for f in range(2):
                options = [jnp.take_along_axis(tile, inner, axis=1) for tile in tiles[f]]
                value = jnp.where(place < 0, options[0], jnp.where(place >= LANES, options[2], options[1]))
                picked[f] = picked[f] + value * share
        own_north = north[:, pl.ds(pl.multiple_of(k * LANES, LANES), LANES)]
        return covered[k] / (picked[1] / total + prior_var), picked[0] / total - north_c * own_north

    def resample(*several):
        values = [resampled(k) for k in several]
        for k, (weight_k, y_k) in zip(several, values):
            part_out[k, 0] = weight_k
            part_out[k, 1] = y_k
        for k in several:

            @pl.when(k != track)
            def _(k=k):
                part(k).start()

    invert(0)
    invert(1)
    edge_out[0, 0] = rates[TILES]
    edge_out[0, 1] = errors[TILES]
    edge_out[1, 0] = rates[1]
    edge_out[1, 1] = errors[1]
    edge_down = side(edge_out.at[0], edge_in.at[0], 2, {"pix": after})
    edge_up = side(edge_out.at[1], edge_in.at[1], 3, {"pix": before})
    edge_down.start()
    edge_up.start()
    invert(2)
    edge_down.wait()
    edge_up.wait()
    for f, field in enumerate((rates, errors)):
        field[0] = jnp.where(row == 0, pltpu.roll(edge_in[0, f], 1, 0), pltpu.roll(field[TILES], 1, 0))
        field[TILES + 1] = jnp.where(
            row == GRD - 1, pltpu.roll(edge_in[1, f], GRD - 1, 0), pltpu.roll(field[1], GRD - 1, 0)
        )
    resample(0)

    def advance(step, carry):
        invert(step)
        resample(step - 2)
        return carry

    lax.fori_loop(3, TILES - 1, advance, 0)
    invert(TILES - 1)
    resample(TILES - 3, TILES - 2, TILES - 1)
    part_in[track] = part_out[track]
    seven = part_in.at[pl.ds(0, TRACKS - 1)]
    pltpu.make_async_copy(seven, seven, part_recv).wait()

    a11 = jnp.full((GRD, LANES), ridge_term, F32)
    a22 = jnp.full((GRD, LANES), ridge_term, F32)
    a12 = jnp.zeros((GRD, LANES), F32)
    b1 = jnp.zeros((GRD, LANES), F32)
    b2 = jnp.zeros((GRD, LANES), F32)
    for t in range(TRACKS):
        w, y = part_in[t, 0], part_in[t, 1]
        e, u = los[0:1, t : t + 1], los[2:3, t : t + 1]
        we, wu = w * e, w * u
        a11, a12, a22 = a11 + we * e, a12 + we * u, a22 + wu * u
        b1, b2 = b1 + we * y, b2 + wu * y
    determ = a11 * a22 - a12 * a12
    east = (a22 * b1 - a12 * b2) / determ
    east_own[...] = east
    sides = [
        side(east_own, east_in.at[0], 4, {"pix": after}),
        side(east_own, east_in.at[1], 5, {"pix": before}),
        side(east_own, east_in.at[2], 6, {"track": right}),
        side(east_own, east_in.at[3], 7, {"track": left}),
    ]
    for copy in sides:
        copy.start()
    result[0] = east
    result[1] = (a11 * b2 - a12 * b1) / determ

    pix_first, pix_last = me == 0, me == PIX - 1
    north_down.wait()
    north_up.wait()
    mine = north_own[...]
    above, below = pltpu.roll(north_in[0], 1, 0), pltpu.roll(north_in[1], GRD - 1, 0)
    above = jnp.where(pix_first, 0.0, above)
    below = jnp.where(pix_last, 0.0, below)
    north_m = jnp.where(row == 0, above, pltpu.roll(mine, 1, 0))
    north_p = jnp.where(row == GRD - 1, below, pltpu.roll(mine, GRD - 1, 0))
    west = north[:, pl.ds(pl.multiple_of(left * LANES, LANES), LANES)]
    orient = north[:, pl.ds(pl.multiple_of(right * LANES, LANES), LANES)]
    west = jnp.where(track == 0, 0.0, pltpu.roll(west, 1, 1))
    orient = jnp.where(track == TRACKS - 1, 0.0, pltpu.roll(orient, LANES - 1, 1))
    north_l = jnp.where(lane == 0, west, pltpu.roll(mine, 1, 1))
    north_r = jnp.where(lane == LANES - 1, orient, pltpu.roll(mine, LANES - 1, 1))
    result[3] = (north_p - north_m) / 2.0

    for copy in sides:
        copy.wait()
    above, below = pltpu.roll(east_in[0], 1, 0), pltpu.roll(east_in[1], GRD - 1, 0)
    above = jnp.where(pix_first, 0.0, above)
    below = jnp.where(pix_last, 0.0, below)
    west = jnp.where(track == 0, 0.0, pltpu.roll(east_in[2], 1, 1))
    orient = jnp.where(track == TRACKS - 1, 0.0, pltpu.roll(east_in[3], LANES - 1, 1))
    east_m = jnp.where(row == 0, above, pltpu.roll(east, 1, 0))
    east_p = jnp.where(row == GRD - 1, below, pltpu.roll(east, GRD - 1, 0))
    east_l = jnp.where(lane == 0, west, pltpu.roll(east, 1, 1))
    east_r = jnp.where(lane == LANES - 1, orient, pltpu.roll(east, LANES - 1, 1))
    result[2] = (east_r - east_l) / 2.0
    result[4] = (east_p - east_m + north_r - north_l) / 4.0

    pltpu.make_async_copy(seven, seven, part_send).wait()
    others = sent.at[:, pl.ds(0, PIX - 1)]
    pltpu.make_async_copy(others, others, send_sem).wait()


def deliver(result, east_up, strain):
    east_up[...] = result[0:2]
    strain[...] = result[2:5]


def per_device(phases, coherent, pairs, res_index, res_weight, coverage, los, north):
    stack = phases[0].reshape(LOCAL, PIX, GRD, TILES, LANES).transpose(1, 2, 3, 0, 4)
    hbm = pl.BlockSpec(memory_space=pl.ANY)
    vmem = pl.BlockSpec(memory_space=pltpu.VMEM)
    dma = pltpu.SemaphoreType.DMA
    width = GRD * GCOLS
    tile = (GRD, LANES)
    result = pl.pallas_call(
        kernel,
        out_shape=jax.ShapeDtypeStruct((5, *tile), F32),
        in_specs=[hbm] * 8,
        out_specs=vmem,
        scratch_shapes=[
            pltpu.VMEM((TILES, PIX, GRD, LOCAL, LANES), BF16),
            pltpu.VMEM((TILES, GRD, PIX, LOCAL, LANES), BF16),
            pltpu.VMEM(coherent.shape[1:], jnp.int32),
            pltpu.VMEM((2, IFGS), jnp.int32),
            pltpu.VMEM((4, width), jnp.int32),
            pltpu.VMEM((4, width), F32),
            pltpu.VMEM((GRD, TILES), jnp.int32),
            pltpu.VMEM((3, TRACKS), F32),
            pltpu.VMEM((GRD, GCOLS), F32),
            pltpu.VMEM((KPAD, KPAD), F32),
            pltpu.VMEM((KPAD, IFGS), BF16),
            pltpu.VMEM((IFGS, KPAD), BF16),
            pltpu.VMEM((IFGS, GCOLS), BF16),
            pltpu.VMEM((TILES + 2, *tile), F32),
            pltpu.VMEM((TILES + 2, *tile), F32),
            pltpu.VMEM((TILES, 4, *tile), jnp.int32),
            pltpu.VMEM((TILES, 4, *tile), F32),
            pltpu.VMEM((TILES, *tile), F32),
            pltpu.VMEM((2, 2, *tile), F32),
            pltpu.VMEM((2, 2, *tile), F32),
            pltpu.VMEM(tile, F32),
            pltpu.VMEM((2, *tile), F32),
            pltpu.VMEM((TRACKS, 2, *tile), F32),
            pltpu.VMEM((TRACKS, 2, *tile), F32),
            pltpu.VMEM(tile, F32),
            pltpu.VMEM((4, *tile), F32),
            dma((TILES,)),
            dma((7,)),
            dma((TILES,)),
            dma(()),
            dma((TILES,)),
            dma((8,)),
            dma((8,)),
            dma(()),
            dma(()),
            pltpu.SemaphoreType.REGULAR,
        ],
        compiler_params=pltpu.CompilerParams(collective_id=0, has_side_effects=True),
    )(stack, coherent[0], pairs[0].T, res_index[0], res_weight[0], coverage[0], los.T, north)
    return pl.pallas_call(
        deliver,
        out_shape=(jax.ShapeDtypeStruct((2, *tile), F32), jax.ShapeDtypeStruct((3, *tile), F32)),
        in_specs=[vmem],
        out_specs=(vmem, vmem),
    )(result)


def solution(mesh):
    in_specs = (
        P("track", "pix", None),
        P("track", "pix", None),
        P("track", None, None),
        P("track", None, "pix"),
        P("track", None, "pix"),
        P("track", "pix", None),
        P(),
        P("pix", None),
    )
    out_specs = (P(None, "pix", "track"), P(None, "pix", "track"))
    return jax.shard_map(
        per_device, mesh=mesh, in_specs=in_specs, out_specs=out_specs, check_vma=False
    )
```
